256 devices in a mesh: feat: 16 (over z, y_lo), cand: 16 (over x, y_hi, core).
Axes of the slice: x: 4, y: 4 (y_hi: 2, y_lo: 2; y = y_hi * 2 + y_lo), z: 8, core: 2. Of those that a mesh axis runs over, the one named last changes fastest.
Arguments:
- cand_grads: bfloat16 [1024, 1048576], P('cand', 'feat'), may hold values from -30 to 30
- val_grads: bfloat16 [256, 1048576], P('cand', 'feat'), may hold values from -30 to 30
- second_moment: float32 [1048576], P('feat'), may hold values from 0.0005 to 1.5
- slot_blocks: int32 [8, 128], replicated, may hold values from 0 to 127, as said below
- slot_seeds: int32 [8, 128], replicated, may hold values from 0 to 1073741823
Outputs:
- scores: float32 [1024, 64], P('cand', 'feat')
The draws below stay inside these ranges and needn't reach their ends.
Inputs may be any that keep to these rules, and one draw needn't show every extreme that they name: `slot_blocks`: each row is a permutation of the input blocks; with L = 128 / (devices of feat), G = (devices of feat) / 8, and o_k = k * G for even k and (k - 1) * G + 1 for odd k, slot k of output block b reads an input block whose index divided by L equals (b / L + o_k) modulo the devices of feat (divisions rounded down).
All inputs are finite; a program needn't handle non-finite values.
Results may differ from the reference program's by a relative error of at most 0.0003.
Values sent between devices are 32-bit elements; how exact they have to be, the bound alone decides.
No kernel may reach another device: no remote copies, remote signals or barrier semaphores. Data moves between devices by JAX's collectives and lax.ppermute only.
A program may use at most 64 MiB of HBM per device.

```python
import math
import jax
import jax.numpy as jnp
from jax import lax

P_SIZE = 1048576
NBLK = 128
PB = 8192
FEATS = 8192
FB = 64
SLOTS = 8
VPT = 4
CANDS = 1024
NVAL = 256
TASKS = 64
N_FEAT = 16


topic_count = 8


def topic_table(key):
    base = jax.random.fold_in(key, 11)
    scale_key = jax.random.fold_in(base, 1)
    noise_key = jax.random.fold_in(base, 2)
    scales = jnp.exp(jax.random.uniform(scale_key, (topic_count, NBLK, 1), jnp.float32, math.log(0.3), math.log(3.0)))
    noise = jnp.clip(jax.random.normal(noise_key, (topic_count, NBLK, PB), jnp.float32), -5.0, 5.0)
    return (noise * scales).reshape(topic_count, P_SIZE)


def mixed_rows_keyed(key, own_key, topics, weights, count):
    table = topic_table(key)
    noise = jnp.clip(jax.random.normal(jax.random.fold_in(own_key, 14), (count, P_SIZE), jnp.float32), -6.0, 6.0)
    return (weights * jnp.take(table, topics, axis=0) + noise).astype(jnp.bfloat16)


def draw_cand_grads(key, part):
    own_key = jax.random.fold_in(key, 21)
    topics = jax.random.randint(jax.random.fold_in(own_key, 12), (CANDS,), 0, topic_count)
    weights = jax.random.uniform(jax.random.fold_in(own_key, 13), (CANDS, 1), jnp.float32, 0.4, 1.6)
    return mixed_rows_keyed(key, own_key, topics, weights, CANDS)


def draw_val_grads(key, part):
    own_key = jax.random.fold_in(key, 22)
    topics = jnp.arange(NVAL, dtype=jnp.int32) // VPT % topic_count
    weights = jax.random.uniform(jax.random.fold_in(own_key, 13), (NVAL, 1), jnp.float32, 0.6, 1.6)
    return mixed_rows_keyed(key, own_key, topics, weights, NVAL)


def draw_second_moment(key, part):
    block_key = jax.random.fold_in(key, 31)
    coord_key = jax.random.fold_in(key, 32)
    levels = jnp.exp(jax.random.uniform(block_key, (NBLK, 1), jnp.float32, math.log(0.001), math.log(1.0)))
    spread = jnp.exp(jax.random.uniform(coord_key, (NBLK, PB), jnp.float32, math.log(0.5), math.log(1.5)))
    return (levels * spread).reshape(P_SIZE)


def draw_slot_blocks(key, part):
    local_count = NBLK // N_FEAT
    stride = N_FEAT // SLOTS
    own_key = jax.random.fold_in(key, 41)
    keys = jax.random.split(own_key, SLOTS * N_FEAT)
    orders = jax.vmap(lambda one_key: jax.random.permutation(one_key, local_count))(keys)
    orders = orders.reshape(SLOTS, N_FEAT, local_count).astype(jnp.int32)
    slot_ids = jnp.arange(SLOTS, dtype=jnp.int32)[:, None]
    odd_part = slot_ids % 2
    offsets = (slot_ids - odd_part) * stride + odd_part
    owners = jnp.arange(N_FEAT, dtype=jnp.int32)[None, :]
    source = (owners + offsets) % N_FEAT
    result = source[:, :, None] * local_count + orders
    return result.reshape(SLOTS, NBLK).astype(jnp.int32)


def place_ends(entries, rng, smallest, top_value):
    index_at = [jax.random.randint(jax.random.fold_in(rng, axis), (), 0, length) for axis, length in enumerate(entries.shape)]
    widest = entries.shape.index(max(entries.shape))
    next_to = index_at[:widest] + [(index_at[widest] + 1) % entries.shape[widest]] + index_at[widest + 1:]
    return entries.at[tuple(index_at)].set(smallest).at[tuple(next_to)].set(top_value)


def setup_inputs(seed: int = 0) -> dict:
    key_list = jax.random.split(jax.random.key(seed), 6)
    cand_grads = draw_cand_grads(jax.random.fold_in(key_list[5], 71), 0)
    val_grads = draw_val_grads(jax.random.fold_in(key_list[5], 71), 0)
    second_moment = draw_second_moment(jax.random.fold_in(key_list[5], 71), 0)
    slot_blocks = draw_slot_blocks(jax.random.fold_in(key_list[5], 71), 0)
    slot_seeds = place_ends(jax.random.randint(key_list[4], (SLOTS, NBLK), 0, 1073741824), jax.random.fold_in(key_list[4], 1), 0, 1073741823).astype(jnp.int32)
    return dict(cand_grads=cand_grads, val_grads=val_grads, second_moment=second_moment, slot_blocks=slot_blocks, slot_seeds=slot_seeds)


def block_signs(seed_val, height, breadth):
    across = lax.broadcasted_iota(jnp.int32, (height, breadth), 0)
    column = lax.broadcasted_iota(jnp.int32, (height, breadth), 1)
    mixed = seed_val ^ across * jnp.int32(73856093) ^ column * jnp.int32(19349663)
    for repeat in range(2):
        mixed = mixed ^ lax.shift_right_logical(mixed, jnp.int32(16))
        mixed = mixed * jnp.int32(73244475)
    mixed = mixed ^ lax.shift_right_logical(mixed, jnp.int32(16))
    return (2 * (mixed & 1) - 1).astype(jnp.float32)

def project(rows_x, slot_blocks, slot_seeds):
    factor = 1.0 / math.sqrt(SLOTS * PB)
    height = rows_x.shape[0]

    def one_block(column):
        summed = jnp.zeros((height, FB), jnp.float32)
        for slot_no in range(SLOTS):
            offset = (slot_blocks[slot_no, column] * PB).astype(jnp.int32)
            segment = lax.dynamic_slice_in_dim(rows_x, offset, PB, 1)
            matrix = (block_signs(slot_seeds[slot_no, column], PB, FB) * factor).astype(jnp.bfloat16)
            summed = summed + jnp.dot(segment, matrix, preferred_element_type=jnp.float32)
        return summed
    blocks = lax.map(one_block, jnp.arange(NBLK, dtype=jnp.int32))
    return jnp.transpose(blocks, (1, 0, 2)).reshape(height, FEATS)

def reference(cand_grads, val_grads, second_moment, slot_blocks, slot_seeds):
    wide = cand_grads.astype(jnp.float32)
    adam_grads = (wide / (jnp.sqrt(0.999 * second_moment[None, :] + 0.001 * wide * wide) + 1e-08)).astype(jnp.bfloat16)
    cand_feats = project(adam_grads, slot_blocks, slot_seeds)
    val_feats = project(val_grads, slot_blocks, slot_seeds)
    cand_norm = jnp.sqrt(lax.optimization_barrier(jnp.sum(cand_feats * cand_feats, axis=1)) + 1e-06)
    val_norm = jnp.sqrt(lax.optimization_barrier(jnp.sum(val_feats * val_feats, axis=1)) + 1e-06)
    val_unit = val_feats / val_norm[:, None]
    dots = jnp.dot(cand_feats, val_unit.T, precision=lax.Precision.HIGHEST)
    cosine = dots / cand_norm[:, None]
    return lax.optimization_barrier(jnp.sum(cosine.reshape(CANDS, TASKS, VPT), axis=2)) / VPT
```

```python
import math

import jax
import jax.numpy as jnp
import numpy as np
from jax import lax
from jax.experimental import pallas as pl
from jax.experimental.pallas import tpu as pltpu
from jax.sharding import PartitionSpec as P

PB = 8192
FEATS = 8192
FB = 64
SLOTS = 8
VPT = 4
CHUNK = 1024


def wrap32(value):
    value &= 0xFFFFFFFF
    return np.int32(value - (1 << 32) if value >= (1 << 31) else value)


MIX = 73244475
ROW_MUL = wrap32(73856093)
COL_MUL = wrap32(19349663)
MIX_A = wrap32(MIX)
MIX_B = wrap32((MIX << 15) + (1 << 31))


def fold(value):
    return value ^ lax.shift_right_logical(value, jnp.int32(16))


def project(slots, adam, seeds_ref, pos_ref, *refs):
    if adam:
        cand_ref, val_ref, moment_ref, out_ref, rows_ref, acc_ref, across_ref, column_ref = refs
    else:
        rows_ref, out_ref, acc_ref, across_ref, column_ref = refs
    step = pl.program_id(0)
    count = len(slots)
    height = rows_ref.shape[0]

    @pl.when(step == 0)
    def _():
        across = lax.broadcasted_iota(jnp.int32, (8, PB), 1) * ROW_MUL
        across_ref[...] = fold(across)
        column = lax.broadcasted_iota(jnp.int32, (FB, 128), 0) * COL_MUL
        column_ref[...] = fold(column)

    mixed = []
    for slot in slots:
        mixed.append(column_ref[...] ^ fold(seeds_ref[slot, step]))
    mixed = jnp.concatenate(mixed, axis=0)

    def one_chunk(chunk, acc):
        at = pl.ds(pl.multiple_of(chunk * CHUNK, CHUNK), CHUNK)
        if adam:
            wide = cand_ref[:, at].astype(jnp.float32)
            moment = 0.999 * moment_ref[:, at]
            square = moment + (0.001 * wide) * wide
            root = lax.rsqrt(square)
            den = square * root + 1e-08
            inverse = root * (2.0 - den * root)
            ncand = cand_ref.shape[0]
            rows_ref[:ncand, at] = (wide * inverse).astype(jnp.bfloat16)
            rows_ref[ncand:, at] = val_ref[:, at]
        across = across_ref[:, at]
        across = jnp.broadcast_to(across[None], (8 * count, 8, CHUNK)).reshape(FB * count, CHUNK)
        value = across ^ jnp.concatenate([mixed] * (CHUNK // 128), axis=1)
        value = fold(value * MIX_A) * MIX_B
        signs = jnp.where(value < 0, jnp.bfloat16(1.0), jnp.bfloat16(-1.0))
        return acc + lax.dot_general(
            signs,
            rows_ref[:, at],
            (((1,), (1,)), ((), ())),
            preferred_element_type=jnp.float32,
        )

    acc = lax.fori_loop(0, PB // CHUNK, one_chunk, jnp.zeros((FB * count, height), jnp.float32))
    for n, slot in enumerate(slots):
        at = pl.multiple_of(pos_ref[slot, step] * FB, FB)
        acc_ref[n, pl.ds(at, FB), :] = acc[n * FB : (n + 1) * FB]

    @pl.when(step == pl.num_programs(0) - 1)
    def _():
        for n in range(count):
            out_ref[n] = acc_ref[n].T


def projected(slots, seeds, pos, operands, adam):
    count = len(slots)
    if adam:
        cand, val, moment = operands
        height = cand.shape[0] + val.shape[0]
        length = cand.shape[1]
        in_specs = [
            pl.BlockSpec((cand.shape[0], PB), lambda i, *_: (0, i)),
            pl.BlockSpec((val.shape[0], PB), lambda i, *_: (0, i)),
            pl.BlockSpec((1, PB), lambda i, *_: (0, i)),
        ]
    else:
        (rows,) = operands
        height, length = rows.shape
        in_specs = [pl.BlockSpec((height, PB), lambda i, *_: (0, i))]
    blocks = length // PB
    width = blocks * FB
    out_shape = [jax.ShapeDtypeStruct((count, height, width), jnp.float32)]
    out_specs = [pl.BlockSpec((count, height, width), lambda i, *_: (0, 0, 0))]
    if adam:
        out_shape.append(jax.ShapeDtypeStruct((height, length), jnp.bfloat16))
        out_specs.append(pl.BlockSpec((height, PB), lambda i, *_: (0, i)))
    return pl.pallas_call(
        lambda *refs: project(slots, adam, *refs),
        out_shape=out_shape,
        grid_spec=pltpu.PrefetchScalarGridSpec(
            num_scalar_prefetch=2,
            grid=(blocks,),
            in_specs=in_specs,
            out_specs=out_specs,
            scratch_shapes=[
                pltpu.VMEM((count, width, height), jnp.float32),
                pltpu.VMEM((8, PB), jnp.int32),
                pltpu.VMEM((FB, 128), jnp.int32),
            ],
        ),
        compiler_params=pltpu.CompilerParams(vmem_limit_bytes=40 << 20),
        cost_estimate=pl.CostEstimate(
            flops=2 * count * width * height * PB * 16,
            bytes_accessed=2 * height * length,
            transcendentals=0,
        ),
        name="project",
    )(seeds, pos, *operands)


def dots_kernel(cand_ref, val_ref, out_ref):
    cand = cand_ref[...]
    val = val_ref[...]
    last = (((1,), (1,)), ((), ()))
    ncand = cand.shape[0]
    dots = lax.dot_general(
        val, cand, last, precision=lax.Precision.HIGHEST, preferred_element_type=jnp.float32
    )
    val_sq = jnp.sum(val * val, axis=1, keepdims=True)
    cand_sq = lax.dot_general(
        jnp.ones((8, cand.shape[1]), jnp.float32),
        cand * cand,
        last,
        precision=lax.Precision.HIGHEST,
        preferred_element_type=jnp.float32,
    )
    shards, _, lanes = out_ref.shape
    own = val.shape[0] // shards
    both = jnp.concatenate([dots, jnp.broadcast_to(val_sq, (val.shape[0], lanes - ncand))], axis=1)
    out_ref[:, :own, :] = both.reshape(shards, own, lanes)
    squares = jnp.concatenate([cand_sq, jnp.zeros((8, lanes - ncand), jnp.float32)], axis=1)
    for shard in range(shards):
        out_ref[shard, own:, :] = squares


def score_kernel(parts_ref, out_ref):
    ncand, ntask = out_ref.shape
    own = ntask * VPT
    total = jnp.sum(parts_ref[...], axis=0)
    val_norm = jnp.sqrt(total[:own, ncand : ncand + 1] + 1e-06)
    cand_norm = jnp.sqrt(total[own : own + 1, :ncand] + 1e-06)
    cosine = total[:own, :ncand] / val_norm / cand_norm
    row = lax.broadcasted_iota(jnp.int32, (own, ntask), 0)
    task = lax.broadcasted_iota(jnp.int32, (own, ntask), 1)
    mean = jnp.where(row // VPT == task, 1.0 / VPT, 0.0)
    out_ref[...] = lax.dot_general(
        cosine,
        mean,
        (((0,), (0,)), ((), ())),
        precision=lax.Precision.HIGHEST,
        preferred_element_type=jnp.float32,
    )


def body(cand_grads, val_grads, second_moment, slot_blocks, slot_seeds):
    devices = lax.axis_size("feat")
    groups = lax.axis_size("cand")
    blocks = second_moment.shape[0] // PB
    first_block = lax.axis_index("feat") * blocks
    factor = 1.0 / math.sqrt(SLOTS * PB)
    stride = devices // SLOTS
    ncand = cand_grads.shape[0]
    nval = val_grads.shape[0]

    local = first_block + lax.broadcasted_iota(jnp.int32, (1, blocks, 1), 1)
    matches = slot_blocks[:, None, :] == local
    seeds = jnp.sum(jnp.where(matches, slot_seeds[:, None, :], 0), axis=2)
    places = lax.broadcasted_iota(jnp.int32, (1, 1, slot_blocks.shape[1]), 2) % blocks
    pos = jnp.sum(jnp.where(matches, places, 0), axis=2)

    def send(part, slot):
        offset = slot * stride if slot % 2 == 0 else (slot - 1) * stride + 1
        pairs = [(j, (j - offset) % devices) for j in range(devices)]
        return lax.ppermute(part, "feat", pairs)

    order = [(4, 5), (2, 3), (6, 7), (1,), (0,)]
    rows = None
    terms = []
    for slots in order:
        if rows is None:
            operands = (cand_grads, val_grads, second_moment[None, :])
            parts, rows = projected(slots, seeds, pos, operands, True)
        else:
            (parts,) = projected(slots, seeds, pos, (rows,), False)
        for n, slot in enumerate(slots):
            terms.append(send(parts[n], slot) if slot else parts[n])
    mine = sum(terms) * factor
    cand_part = mine[:ncand]
    val_part = mine[ncand:]
    val_all = lax.all_to_all(
        jnp.broadcast_to(val_part[None], (groups, *val_part.shape)), "cand", 0, 0, tiled=True
    )
    val_all = val_all.reshape(groups * nval, val_part.shape[1])
    own = groups * nval // devices
    packed = pl.pallas_call(
        dots_kernel,
        out_shape=jax.ShapeDtypeStruct((devices, own + 8, 128), jnp.float32),
        name="dots",
    )(cand_part, val_all)
    parts = lax.all_to_all(packed, "feat", 0, 0, tiled=True)
    return pl.pallas_call(
        score_kernel,
        out_shape=jax.ShapeDtypeStruct((ncand, own // VPT), jnp.float32),
        name="score",
    )(parts)


def solution(mesh):
    placed = (P("cand", "feat"), P("cand", "feat"), P("feat"), P(), P())
    return jax.shard_map(
        body, mesh=mesh, in_specs=placed, out_specs=P("cand", "feat"), check_vma=False
    )
```

```python
import math

import jax
import jax.numpy as jnp
import numpy as np
from jax import lax
from jax.experimental import pallas as pl
from jax.experimental.pallas import tpu as pltpu
from jax.sharding import PartitionSpec as P


PB = 8192
FB = 64
SLOTS = 8
VPT = 4
GRANT = 62 << 20
AHEAD = 2
ORDER = ((4, 5, 2, 3), (6, 7, 1), (0,))


def wrap32(value):
    value &= 0xFFFFFFFF
    return np.int32(value - (1 << 32) if value >= (1 << 31) else value)


MIX = 73244475
ROW_MUL = wrap32(73856093)
COL_MUL = wrap32(19349663)
MIX_A = wrap32(MIX)
MIX_B = wrap32((MIX << 15) + (1 << 31))


def fold(value):
    return value ^ lax.shift_right_logical(value, jnp.int32(16))


def offset_of(slot, stride):
    return slot * stride if slot % 2 == 0 else (slot - 1) * stride + 1


def project(slots, adam, devices, me_ref, blocks_ref, seeds_ref, *refs):
    if adam:
        cand_hbm, val_hbm, moment_hbm, *out_refs = refs
        *out_refs, rows_hbm, rows_ref, acc_ref, table_ref, sem, cand_ref, moment_ref = out_refs
    else:
        rows_hbm, *out_refs = refs
        *out_refs, rows_ref, acc_ref, table_ref, sem = out_refs
    count = len(slots)
    height, length = rows_ref.shape
    blocks = length // PB

    def copies(block):
        at = pl.ds(pl.multiple_of(block * PB, PB), PB)
        if not adam:
            return (pltpu.make_async_copy(rows_hbm.at[:, at], rows_ref.at[:, at], sem.at[0, block]),)
        ncand = cand_ref.shape[0]
        return (
            pltpu.make_async_copy(moment_hbm.at[:, at], moment_ref.at[:, at], sem.at[0, block]),
            pltpu.make_async_copy(cand_hbm.at[:, at], cand_ref.at[:, at], sem.at[1, block]),
            pltpu.make_async_copy(val_hbm.at[:, at], rows_ref.at[ncand:, at], sem.at[2, block]),
        )

    def copy_out(block):
        at = pl.ds(pl.multiple_of(block * PB, PB), PB)
        return pltpu.make_async_copy(rows_ref.at[:, at], rows_hbm.at[:, at], sem.at[3, block])

    for block in range(AHEAD):
        for copy in copies(block):
            copy.start()
    me = me_ref[0]
    for n, slot in enumerate(slots):
        owner = lax.rem(me + devices - offset_of(slot, devices // SLOTS), devices)
        for place in range(blocks):
            source = blocks_ref[slot, owner * blocks + place] - me * blocks
            table_ref[0, n, source] = seeds_ref[slot, owner * blocks + place]
            table_ref[1, n, source] = place
    across = fold(lax.broadcasted_iota(jnp.int32, (8, PB), 1) * ROW_MUL)
    column = fold(lax.broadcasted_iota(jnp.int32, (FB, 128), 0) * COL_MUL)
    lane_half = lax.broadcasted_iota(jnp.int32, (height, 2 * FB), 1) // FB

    def one_block(block, carry):
        at = pl.ds(pl.multiple_of(block * PB, PB), PB)

        @pl.when(block + AHEAD < blocks)
        def _():
            for copy in copies(block + AHEAD):
                copy.start()

        for copy in copies(block):
            copy.wait()
        if adam:
            wide = cand_ref[:, at].astype(jnp.float32)
            square = 0.999 * moment_ref[:, at] + (0.001 * wide) * wide
            den = square * lax.rsqrt(square) + 1e-08
            rows_ref[: cand_ref.shape[0], at] = (wide * lax.rsqrt(den * den)).astype(jnp.bfloat16)
            copy_out(block).start()
        mixed = []
        for n in range(count):
            mixed.append(column ^ fold(table_ref[0, n, block]))
        mixed = jnp.concatenate(mixed, axis=0)
        value = jnp.broadcast_to(across[None], (8 * count, 8, PB)).reshape(FB * count, PB)
        value = value ^ jnp.concatenate([mixed] * (PB // 128), axis=1)
        value = fold(value * MIX_A) * MIX_B
        signs = jnp.where(value < 0, jnp.bfloat16(1.0), jnp.bfloat16(-1.0))
        acc = lax.dot_general(
            rows_ref[:, at],
            signs,
            (((1,), (1,)), ((), ())),
            preferred_element_type=jnp.float32,
        )
        if count % 2:
            acc = jnp.concatenate([acc, jnp.zeros((height, FB), jnp.float32)], axis=1)
        for n in range(count):
            place = table_ref[1, n, block]
            half = place % 2
            pair = n // 2 * 2 * FB
            moved = pltpu.roll(acc[:, pair : pair + 2 * FB], (half ^ (n % 2)) * FB, 1)
            acc_ref[n, place // 2] = jnp.where(lane_half == half, moved, acc_ref[n, place // 2])
        return carry

    lax.fori_loop(0, blocks, one_block, 0)
    for n in range(count):
        for pair in range(acc_ref.shape[1]):
            out_refs[n][:, pair * 2 * FB : (pair + 1) * 2 * FB] = acc_ref[n, pair]
    if adam:
        for block in range(blocks):
            copy_out(block).wait()


def projected(slots, tables, operands, adam, devices):
    count = len(slots)
    smem = pl.BlockSpec(memory_space=pltpu.SMEM)
    vmem = pl.BlockSpec(memory_space=pltpu.VMEM)
    if adam:
        cand, val, moment = operands
        height = cand.shape[0] + val.shape[0]
        length = cand.shape[1]
    else:
        (rows,) = operands
        height, length = rows.shape
    blocks = length // PB
    width = blocks * FB
    out_shape = [jax.ShapeDtypeStruct((height, width), jnp.float32)] * count
    out_specs = [vmem] * count
    scratch = [
        pltpu.VMEM((height, length), jnp.bfloat16),
        pltpu.VMEM((count, width // (2 * FB), height, 2 * FB), jnp.float32),
        pltpu.SMEM((2, count, blocks), jnp.int32),
        pltpu.SemaphoreType.DMA((4, blocks)),
    ]
    if adam:
        out_shape.append(jax.ShapeDtypeStruct((height, length), jnp.bfloat16))
        out_specs.append(pl.BlockSpec(memory_space=pl.ANY))
        scratch += [
            pltpu.VMEM(cand.shape, jnp.bfloat16),
            pltpu.VMEM(moment.shape, jnp.float32),
        ]
    return pl.pallas_call(
        lambda *refs: project(slots, adam, devices, *refs),
        out_shape=out_shape,
        in_specs=[smem, smem, smem] + [pl.BlockSpec(memory_space=pl.ANY)] * len(operands),
        out_specs=out_specs,
        scratch_shapes=scratch,
        compiler_params=pltpu.CompilerParams(vmem_limit_bytes=GRANT),
        cost_estimate=pl.CostEstimate(
            flops=2 * count * width * height * PB * 16,
            bytes_accessed=2 * height * length,
            transcendentals=0,
        ),
        name="project",
    )(*tables, *operands)


def merge_kernel(*refs):
    *term_refs, cand_ref, val_ref = refs
    total = term_refs[0][...]
    for term_ref in term_refs[1:]:
        total = total + term_ref[...]
    total = total * (1.0 / math.sqrt(SLOTS * PB))
    ncand = cand_ref.shape[0]
    cand_ref[...] = total[:ncand]
    val_ref[...] = jnp.broadcast_to(total[None, ncand:], val_ref.shape)


def dots_kernel(core_ref, cand_ref, own_ref, other_ref, out_ref):
    cand = cand_ref[...]
    last = (((1,), (1,)), ((), ()))
    ncand = cand.shape[0]
    groups, cores, _, lanes = out_ref.shape
    nval = own_ref.shape[1]
    cand_sq = lax.dot_general(
        jnp.ones((8, cand.shape[1]), jnp.float32),
        cand * cand,
        last,
        precision=lax.Precision.HIGHEST,
        preferred_element_type=jnp.float32,
    )
    squares = jnp.concatenate([cand_sq, jnp.zeros((8, lanes - ncand), jnp.float32)], axis=1)
    val = jnp.concatenate(
        [ref[...].reshape(groups * nval, ref.shape[2]) for ref in (own_ref, other_ref)], axis=0
    )
    dots = lax.dot_general(
        val, cand, last, precision=lax.Precision.HIGHEST, preferred_element_type=jnp.float32
    )
    val_sq = jnp.sum(val * val, axis=1, keepdims=True)
    both = jnp.concatenate([dots, jnp.broadcast_to(val_sq, (val.shape[0], lanes - ncand))], axis=1)
    for swapped in range(cores):
        core = core_ref[0] ^ swapped
        for group in range(groups):
            at = (swapped * groups + group) * nval
            out_ref[group, core, :nval, :] = both[at : at + nval]
            out_ref[group, core, nval:, :] = squares


def score_kernel(parts_ref, out_ref):
    ntask, ncand = out_ref.shape
    own = ntask * VPT
    total = jnp.sum(parts_ref[...], axis=0)
    val_norm = jnp.sqrt(total[:own, ncand : ncand + 1] + 1e-06)
    cand_norm = jnp.sqrt(total[own : own + 1, :ncand] + 1e-06)
    cosine = total[:own, :ncand] / val_norm / cand_norm
    rows = [
        jnp.sum(cosine[task * VPT : (task + 1) * VPT], axis=0, keepdims=True) for task in range(ntask)
    ]
    out_ref[...] = jnp.concatenate(rows, axis=0) / VPT


def body(cand_grads, val_grads, second_moment, slot_blocks, slot_seeds):
    devices = lax.axis_size("feat")
    groups = lax.axis_size("cand")
    ncand = cand_grads.shape[0]
    nval = val_grads.shape[0]

    tables = (lax.axis_index("feat").reshape(1), slot_blocks, slot_seeds)

    def send(part, slot):
        offset = offset_of(slot, devices // SLOTS)
        pairs = [(j, (j - offset) % devices) for j in range(devices)]
        return lax.ppermute(part, "feat", pairs)

    rows = None
    terms = []
    for slots in ORDER:
        if rows is None:
            operands = (cand_grads, val_grads, second_moment[None, :])
            *parts, rows = projected(slots, tables, operands, True, devices)
        else:
            parts = projected(slots, tables, (rows,), False, devices)
        for part, slot in zip(parts, slots):
            terms.append(send(part, slot) if slot else part)
    small = pltpu.CompilerParams(vmem_limit_bytes=8 << 20)
    pairs = groups // 2
    width = terms[0].shape[1]
    cand_part, val_part = pl.pallas_call(
        merge_kernel,
        out_shape=[
            jax.ShapeDtypeStruct((ncand, width), jnp.float32),
            jax.ShapeDtypeStruct((pairs, nval, width), jnp.float32),
        ],
        compiler_params=small,
        name="merge",
    )(*terms)
    same_core = [[2 * m + core for m in range(pairs)] for core in range(2)]
    val_own = lax.all_to_all(
        val_part, "cand", 0, 0, tiled=True, axis_index_groups=same_core
    )
    val_other = lax.ppermute(val_own, "cand", [(c, c ^ 1) for c in range(groups)])
    own = groups * nval // devices
    packed = pl.pallas_call(
        dots_kernel,
        out_shape=jax.ShapeDtypeStruct((pairs, 2, own + 8, 128), jnp.float32),
        in_specs=[pl.BlockSpec(memory_space=pltpu.SMEM)] + [pl.BlockSpec()] * 3,
        compiler_params=small,
        name="dots",
    )((lax.axis_index("cand") % 2).reshape(1), cand_part, val_own, val_other)
    packed = packed.reshape(devices, own + 8, 128)
    parts = lax.all_to_all(packed, "feat", 0, 0, tiled=True)
    return pl.pallas_call(
        score_kernel,
        out_shape=jax.ShapeDtypeStruct((own // VPT, ncand), jnp.float32),
        compiler_params=small,
        name="score",
    )(parts).T


def solution(mesh):
    placed = (P("cand", "feat"), P("cand", "feat"), P("feat"), P(), P())
    return jax.shard_map(
        body, mesh=mesh, in_specs=placed, out_specs=P("cand", "feat"), check_vma=False
    )
```

```python
import math

import jax
import jax.numpy as jnp
import numpy as np
from jax import lax
from jax.experimental import pallas as pl
from jax.experimental.pallas import tpu as pltpu
from jax.sharding import PartitionSpec as P


PB = 8192
FB = 64
SLOTS = 8
VPT = 4
GRANT = 32 << 20
SMALL_GRANT = 16 << 20
AHEAD = 2


def wrap32(value):
    value &= 0xFFFFFFFF
    return np.int32(value - (1 << 32) if value >= (1 << 31) else value)


MIX = 73244475
ROW_MUL = wrap32(73856093)
COL_MUL = wrap32(19349663)
MIX_A = wrap32(MIX)
MIX_B = wrap32((MIX << 15) + (1 << 31))


def fold(value):
    return value ^ lax.shift_right_logical(value, jnp.int32(16))


def offset_of(slot, stride):
    return slot * stride if slot % 2 == 0 else (slot - 1) * stride + 1


def project(slots, adam, devices, me_ref, blocks_ref, seeds_ref, *refs):
    if adam:
        cand_hbm, val_hbm, moment_hbm, out_ref, rows_ref, acc_ref, table_ref, cand_ref, moment_ref, sem = refs
    else:
        rows_ref, out_ref, acc_ref, table_ref = refs
    count = len(slots)
    height, length = rows_ref.shape
    blocks = length // PB

    def copies(block):
        at = pl.ds(pl.multiple_of(block * PB, PB), PB)
        ncand = cand_ref.shape[0]
        return (
            pltpu.make_async_copy(moment_hbm.at[:, at], moment_ref.at[:, at], sem.at[0, block]),
            pltpu.make_async_copy(cand_hbm.at[:, at], cand_ref.at[:, at], sem.at[1, block]),
            pltpu.make_async_copy(val_hbm.at[:, at], rows_ref.at[ncand:, at], sem.at[2, block]),
        )

    if adam:
        for block in range(AHEAD):
            for copy in copies(block):
                copy.start()
    me = me_ref[0]
    for n, slot in enumerate(slots):
        owner = lax.rem(me + devices - offset_of(slot, devices // SLOTS), devices)
        for place in range(blocks):
            source = blocks_ref[slot, owner * blocks + place] - me * blocks
            table_ref[0, n, source] = seeds_ref[slot, owner * blocks + place]
            table_ref[1, n, source] = place
    across = fold(lax.broadcasted_iota(jnp.int32, (8, PB), 1) * ROW_MUL)
    column = fold(lax.broadcasted_iota(jnp.int32, (FB, 128), 0) * COL_MUL)
    lane_half = lax.broadcasted_iota(jnp.int32, (height, 2 * FB), 1) // FB

    def one_block(block, carry):
        at = pl.ds(pl.multiple_of(block * PB, PB), PB)
        if adam:

            @pl.when(block + AHEAD < blocks)
            def _():
                for copy in copies(block + AHEAD):
                    copy.start()

            for copy in copies(block):
                copy.wait()
            wide = cand_ref[:, at].astype(jnp.float32)
            square = 0.999 * moment_ref[:, at] + (0.001 * wide) * wide
            den = square * lax.rsqrt(square) + 1e-08
            rows_ref[: cand_ref.shape[0], at] = (wide * lax.rsqrt(den * den)).astype(jnp.bfloat16)
        mixed = []
        for n in range(count):
            mixed.append(column ^ fold(table_ref[0, n, block]))
        mixed = jnp.concatenate(mixed, axis=0)
        value = jnp.broadcast_to(across[None], (8 * count, 8, PB)).reshape(FB * count, PB)
        value = value ^ jnp.concatenate([mixed] * (PB // 128), axis=1)
        value = fold(value * MIX_A) * MIX_B
        signs = jnp.where(value < 0, jnp.bfloat16(1.0), jnp.bfloat16(-1.0))
        acc = lax.dot_general(
            rows_ref[:, at],
            signs,
            (((1,), (1,)), ((), ())),
            preferred_element_type=jnp.float32,
        )
        if count % 2:
            acc = jnp.concatenate([acc, jnp.zeros((height, FB), jnp.float32)], axis=1)
        for n in range(count):
            place = table_ref[1, n, block]
            half = place % 2
            pair = n // 2 * 2 * FB
            moved = pltpu.roll(acc[:, pair : pair + 2 * FB], (half ^ (n % 2)) * FB, 1)
            acc_ref[n, place // 2] = jnp.where(lane_half == half, moved, acc_ref[n, place // 2])
        return carry

    lax.fori_loop(0, blocks, one_block, 0)
    for n in range(count):
        for pair in range(acc_ref.shape[1]):
            out_ref[n, :, pair * 2 * FB : (pair + 1) * 2 * FB] = acc_ref[n, pair]


def projected(slots, tables, operands, adam, devices):
    count = len(slots)
    smem = pl.BlockSpec(memory_space=pltpu.SMEM)
    vmem = pl.BlockSpec(memory_space=pltpu.VMEM)
    if adam:
        cand, val, moment = operands
        height = cand.shape[0] + val.shape[0]
        length = cand.shape[1]
    else:
        (rows,) = operands
        height, length = rows.shape
    blocks = length // PB
    width = blocks * FB
    out_shape = [jax.ShapeDtypeStruct((count, height, width), jnp.float32)]
    out_specs = [vmem]
    scratch = [
        pltpu.VMEM((count, width // (2 * FB), height, 2 * FB), jnp.float32),
        pltpu.SMEM((2, count, blocks), jnp.int32),
    ]
    if adam:
        out_shape.append(jax.ShapeDtypeStruct((height, length), jnp.bfloat16))
        out_specs.append(vmem)
        scratch += [
            pltpu.VMEM(cand.shape, jnp.bfloat16),
            pltpu.VMEM(moment.shape, jnp.float32),
            pltpu.SemaphoreType.DMA((3, blocks)),
        ]
    return pl.pallas_call(
        lambda *refs: project(slots, adam, devices, *refs),
        out_shape=out_shape,
        in_specs=[smem, smem, smem] + [pl.BlockSpec(memory_space=pltpu.HBM) if adam else vmem] * len(operands),
        out_specs=out_specs,
        scratch_shapes=scratch,
        compiler_params=pltpu.CompilerParams(vmem_limit_bytes=GRANT if adam else SMALL_GRANT),
        cost_estimate=pl.CostEstimate(
            flops=2 * count * width * height * PB * 16,
            bytes_accessed=2 * height * length,
            transcendentals=0,
        ),
        name="project",
    )(*tables, *operands)


def join_kernel(odd_ref, even_ref, *out_refs):
    for n, out_ref in enumerate(out_refs):
        out_ref[...] = odd_ref[n + 1] + even_ref[n]


def merge_kernel(odd_ref, kept_ref, first_ref, second_ref, third_ref, cand_ref, val_ref):
    total = (odd_ref[0] + kept_ref[0]) + (first_ref[...] + second_ref[...]) + third_ref[...]
    total = total * (1.0 / math.sqrt(SLOTS * PB))
    ncand = cand_ref.shape[0]
    cand_ref[...] = total[:ncand]
    val_ref[...] = jnp.broadcast_to(total[None, ncand:], val_ref.shape)


def dots_kernel(core_ref, cand_ref, own_ref, other_ref, out_ref):
    cand = cand_ref[...]
    last = (((1,), (1,)), ((), ()))
    ncand = cand.shape[0]
    groups, cores, _, lanes = out_ref.shape
    nval = own_ref.shape[1]
    cand_sq = lax.dot_general(
        jnp.ones((8, cand.shape[1]), jnp.float32),
        cand * cand,
        last,
        precision=lax.Precision.HIGHEST,
        preferred_element_type=jnp.float32,
    )
    squares = jnp.concatenate([cand_sq, jnp.zeros((8, lanes - ncand), jnp.float32)], axis=1)
    val = jnp.concatenate(
        [ref[...].reshape(groups * nval, ref.shape[2]) for ref in (own_ref, other_ref)], axis=0
    )
    dots = lax.dot_general(
        val, cand, last, precision=lax.Precision.HIGHEST, preferred_element_type=jnp.float32
    )
    val_sq = jnp.sum(val * val, axis=1, keepdims=True)
    both = jnp.concatenate([dots, jnp.broadcast_to(val_sq, (val.shape[0], lanes - ncand))], axis=1)
    for swapped in range(cores):
        core = core_ref[0] ^ swapped
        for group in range(groups):
            at = (swapped * groups + group) * nval
            out_ref[group, core, :nval, :] = both[at : at + nval]
            out_ref[group, core, nval:, :] = squares


def score_kernel(parts_ref, out_ref):
    ntask, ncand = out_ref.shape
    own = ntask * VPT
    total = jnp.sum(parts_ref[...], axis=0)
    val_norm = jnp.sqrt(total[:own, ncand : ncand + 1] + 1e-06)
    cand_norm = jnp.sqrt(total[own : own + 1, :ncand] + 1e-06)
    cosine = total[:own, :ncand] / val_norm / cand_norm
    rows = [
        jnp.sum(cosine[task * VPT : (task + 1) * VPT], axis=0, keepdims=True) for task in range(ntask)
    ]
    out_ref[...] = jnp.concatenate(rows, axis=0) / VPT


def body(cand_grads, val_grads, second_moment, slot_blocks, slot_seeds):
    devices = lax.axis_size("feat")
    groups = lax.axis_size("cand")
    ncand = cand_grads.shape[0]
    nval = val_grads.shape[0]

    cand_grads, val_grads, second_moment, slot_blocks, slot_seeds = (
        pltpu.with_memory_space_constraint(x, pltpu.HBM)
        for x in (cand_grads, val_grads, second_moment[None, :], slot_blocks, slot_seeds)
    )
    tables = (lax.axis_index("feat").reshape(1), slot_blocks, slot_seeds)

    def back(part, steps):
        return lax.ppermute(part, "feat", [(j, (j - steps) % devices) for j in range(devices)])

    apart = devices // (SLOTS // 2)
    small = pltpu.CompilerParams(vmem_limit_bytes=8 << 20)
    operands = (cand_grads, val_grads, second_moment)
    odd, rows = projected((1, 3, 5, 7), tables, operands, True, devices)
    odd = back(odd, 1)
    (even,) = projected((2, 4, 6), tables, (rows,), False, devices)
    joined = pl.pallas_call(
        join_kernel,
        out_shape=[jax.ShapeDtypeStruct(even.shape[1:], jnp.float32)] * 3,
        compiler_params=small,
        name="join",
    )(odd, even)
    second = back(joined[1], 2 * apart)
    first = back(joined[0], apart)
    third = back(joined[2], 3 * apart)
    (kept,) = projected((0,), tables, (rows,), False, devices)

    pairs = groups // 2
    width = first.shape[1]
    cand_part, val_part = pl.pallas_call(
        merge_kernel,
        out_shape=[
            jax.ShapeDtypeStruct((ncand, width), jnp.float32),
            jax.ShapeDtypeStruct((pairs, nval, width), jnp.float32),
        ],
        compiler_params=small,
        name="merge",
    )(odd, kept, first, second, third)
    same_core = [[2 * m + core for m in range(pairs)] for core in range(2)]
    val_own = lax.all_to_all(
        val_part, "cand", 0, 0, tiled=True, axis_index_groups=same_core
    )
    val_other = lax.ppermute(val_own, "cand", [(c, c ^ 1) for c in range(groups)])
    own = groups * nval // devices
    packed = pl.pallas_call(
        dots_kernel,
        out_shape=jax.ShapeDtypeStruct((pairs, 2, own + 8, 128), jnp.float32),
        in_specs=[pl.BlockSpec(memory_space=pltpu.SMEM)] + [pl.BlockSpec()] * 3,
        compiler_params=small,
        name="dots",
    )((lax.axis_index("cand") % 2).reshape(1), cand_part, val_own, val_other)
    packed = packed.reshape(devices, own + 8, 128)
    parts = lax.all_to_all(packed, "feat", 0, 0, tiled=True)
    return pl.pallas_call(
        score_kernel,
        out_shape=jax.ShapeDtypeStruct((own // VPT, ncand), jnp.float32),
        compiler_params=small,
        name="score",
    )(parts).T


def solution(mesh):
    placed = (P("cand", "feat"), P("cand", "feat"), P("feat"), P(), P())
    return jax.shard_map(
        body, mesh=mesh, in_specs=placed, out_specs=P("cand", "feat"), check_vma=False
    )
```

```python
import math

import jax
import jax.numpy as jnp
import numpy as np
from jax import lax
from jax.experimental import pallas as pl
from jax.experimental.pallas import tpu as pltpu
from jax.sharding import PartitionSpec as P


PB = 8192
FB = 64
SLOTS = 8
VPT = 4
GRANT = 32 << 20
SMALL_GRANT = 16 << 20
AHEAD = 2


def wrap32(value):
    value &= 0xFFFFFFFF
    return np.int32(value - (1 << 32) if value >= (1 << 31) else value)


MIX = 73244475
ROW_MUL = wrap32(73856093)
COL_MUL = wrap32(19349663)
MIX_A = wrap32(MIX)
MIX_B = wrap32((MIX << 15) + (1 << 31))


def fold(value):
    return value ^ lax.shift_right_logical(value, jnp.int32(16))


def offset_of(slot, stride):
    return slot * stride if slot % 2 == 0 else (slot - 1) * stride + 1


def project(slots, adam, devices, me_ref, blocks_ref, seeds_ref, *refs):
    if adam:
        cand_hbm, val_hbm, moment_hbm, out_ref, rows_ref, acc_ref, table_ref, cand_ref, moment_ref, sem = refs
    else:
        rows_ref, out_ref, acc_ref, table_ref = refs
    count = len(slots)
    height, length = rows_ref.shape
    blocks = length // PB

    def copies(block):
        at = pl.ds(pl.multiple_of(block * PB, PB), PB)
        ncand = cand_ref.shape[0]
        return (
            pltpu.make_async_copy(moment_hbm.at[:, at], moment_ref.at[:, at], sem.at[0, block]),
            pltpu.make_async_copy(cand_hbm.at[:, at], cand_ref.at[:, at], sem.at[1, block]),
            pltpu.make_async_copy(val_hbm.at[:, at], rows_ref.at[ncand:, at], sem.at[2, block]),
        )

    if adam:
        for block in range(AHEAD):
            for copy in copies(block):
                copy.start()
    me = me_ref[0]
    for n, slot in enumerate(slots):
        owner = lax.rem(me + devices - offset_of(slot, devices // SLOTS), devices)
        for place in range(blocks):
            source = blocks_ref[slot, owner * blocks + place] - me * blocks
            table_ref[0, n, source] = seeds_ref[slot, owner * blocks + place]
            table_ref[1, n, source] = place
    across = fold(lax.broadcasted_iota(jnp.int32, (8, PB), 1) * ROW_MUL)
    column = fold(lax.broadcasted_iota(jnp.int32, (FB, 128), 0) * COL_MUL)
    lane_half = lax.broadcasted_iota(jnp.int32, (height, 2 * FB), 1) // FB

    def one_block(block, carry):
        at = pl.ds(pl.multiple_of(block * PB, PB), PB)
        if adam:

            @pl.when(block + AHEAD < blocks)
            def _():
                for copy in copies(block + AHEAD):
                    copy.start()

            for copy in copies(block):
                copy.wait()
            wide = cand_ref[:, at].astype(jnp.float32)
            square = 0.999 * moment_ref[:, at] + (0.001 * wide) * wide
            den = square * lax.rsqrt(square) + 1e-08
            rows_ref[: cand_ref.shape[0], at] = (wide * lax.rsqrt(den * den)).astype(jnp.bfloat16)
        mixed = []
        for n in range(count):
            mixed.append(column ^ fold(table_ref[0, n, block]))
        mixed = jnp.concatenate(mixed, axis=0)
        value = jnp.broadcast_to(across[None], (8 * count, 8, PB)).reshape(FB * count, PB)
        value = value ^ jnp.concatenate([mixed] * (PB // 128), axis=1)
        value = fold(value * MIX_A) * MIX_B
        signs = jnp.where(value < 0, jnp.bfloat16(1.0), jnp.bfloat16(-1.0))
        acc = lax.dot_general(
            rows_ref[:, at],
            signs,
            (((1,), (1,)), ((), ())),
            preferred_element_type=jnp.float32,
        )
        if count % 2:
            acc = jnp.concatenate([acc, jnp.zeros((height, FB), jnp.float32)], axis=1)
        for n in range(count):
            place = table_ref[1, n, block]
            half = place % 2
            pair = n // 2 * 2 * FB
            moved = pltpu.roll(acc[:, pair : pair + 2 * FB], (half ^ (n % 2)) * FB, 1)
            acc_ref[n, place // 2] = jnp.where(lane_half == half, moved, acc_ref[n, place // 2])
        return carry

    lax.fori_loop(0, blocks, one_block, 0)
    for n in range(count):
        for pair in range(acc_ref.shape[1]):
            out_ref[n, :, pair * 2 * FB : (pair + 1) * 2 * FB] = acc_ref[n, pair]


def projected(slots, tables, operands, adam, devices):
    count = len(slots)
    smem = pl.BlockSpec(memory_space=pltpu.SMEM)
    vmem = pl.BlockSpec(memory_space=pltpu.VMEM)
    if adam:
        cand, val, moment = operands
        height = cand.shape[0] + val.shape[0]
        length = cand.shape[1]
    else:
        (rows,) = operands
        height, length = rows.shape
    blocks = length // PB
    width = blocks * FB
    out_shape = [jax.ShapeDtypeStruct((count, height, width), jnp.float32)]
    out_specs = [vmem]
    scratch = [
        pltpu.VMEM((count, width // (2 * FB), height, 2 * FB), jnp.float32),
        pltpu.SMEM((2, count, blocks), jnp.int32),
    ]
    if adam:
        out_shape.append(jax.ShapeDtypeStruct((height, length), jnp.bfloat16))
        out_specs.append(vmem)
        scratch += [
            pltpu.VMEM(cand.shape, jnp.bfloat16),
            pltpu.VMEM(moment.shape, jnp.float32),
            pltpu.SemaphoreType.DMA((3, blocks)),
        ]
    return pl.pallas_call(
        lambda *refs: project(slots, adam, devices, *refs),
        out_shape=out_shape,
        in_specs=[smem, smem, smem] + [pl.BlockSpec(memory_space=pltpu.HBM) if adam else vmem] * len(operands),
        out_specs=out_specs,
        scratch_shapes=scratch,
        compiler_params=pltpu.CompilerParams(vmem_limit_bytes=GRANT if adam else SMALL_GRANT),
        cost_estimate=pl.CostEstimate(
            flops=2 * count * width * height * PB * 16,
            bytes_accessed=2 * height * length,
            transcendentals=0,
        ),
        name="project",
    )(*tables, *operands)


def join_kernel(odd_ref, even_ref, *out_refs):
    for n, out_ref in enumerate(out_refs):
        out_ref[...] = odd_ref[n] + even_ref[n]


def merge_kernel(*refs):
    *term_refs, cand_ref, val_ref = refs
    total = term_refs[0][...]
    for term_ref in term_refs[1:]:
        total = total + term_ref[...]
    total = total * (1.0 / math.sqrt(SLOTS * PB))
    ncand = cand_ref.shape[0]
    cand_ref[...] = total[:ncand]
    val_ref[...] = jnp.broadcast_to(total[None, ncand:], val_ref.shape)


def dots_kernel(core_ref, cand_ref, own_ref, other_ref, out_ref):
    cand = cand_ref[...]
    last = (((1,), (1,)), ((), ()))
    ncand = cand.shape[0]
    groups, cores, _, lanes = out_ref.shape
    nval = own_ref.shape[1]
    cand_sq = lax.dot_general(
        jnp.ones((8, cand.shape[1]), jnp.float32),
        cand * cand,
        last,
        precision=lax.Precision.HIGHEST,
        preferred_element_type=jnp.float32,
    )
    squares = jnp.concatenate([cand_sq, jnp.zeros((8, lanes - ncand), jnp.float32)], axis=1)
    val = jnp.concatenate(
        [ref[...].reshape(groups * nval, ref.shape[2]) for ref in (own_ref, other_ref)], axis=0
    )
    dots = lax.dot_general(
        val, cand, last, precision=lax.Precision.HIGHEST, preferred_element_type=jnp.float32
    )
    val_sq = jnp.sum(val * val, axis=1, keepdims=True)
    both = jnp.concatenate([dots, jnp.broadcast_to(val_sq, (val.shape[0], lanes - ncand))], axis=1)
    for swapped in range(cores):
        core = core_ref[0] ^ swapped
        for group in range(groups):
            at = (swapped * groups + group) * nval
            out_ref[group, core, :nval, :] = both[at : at + nval]
            out_ref[group, core, nval:, :] = squares


def score_kernel(parts_ref, out_ref):
    ntask, ncand = out_ref.shape
    own = ntask * VPT
    total = jnp.sum(parts_ref[...], axis=0)
    val_norm = jnp.sqrt(total[:own, ncand : ncand + 1] + 1e-06)
    cand_norm = jnp.sqrt(total[own : own + 1, :ncand] + 1e-06)
    cosine = total[:own, :ncand] / val_norm / cand_norm
    rows = [
        jnp.sum(cosine[task * VPT : (task + 1) * VPT], axis=0, keepdims=True) for task in range(ntask)
    ]
    out_ref[...] = jnp.concatenate(rows, axis=0) / VPT


def body(cand_grads, val_grads, second_moment, slot_blocks, slot_seeds):
    devices = lax.axis_size("feat")
    groups = lax.axis_size("cand")
    ncand = cand_grads.shape[0]
    nval = val_grads.shape[0]

    cand_grads, val_grads, second_moment, slot_blocks, slot_seeds = (
        pltpu.with_memory_space_constraint(x, pltpu.HBM)
        for x in (cand_grads, val_grads, second_moment[None, :], slot_blocks, slot_seeds)
    )
    tables = (lax.axis_index("feat").reshape(1), slot_blocks, slot_seeds)

    def back(part, steps):
        return lax.ppermute(part, "feat", [(j, (j - steps) % devices) for j in range(devices)])

    apart = devices // (SLOTS // 2)
    small = pltpu.CompilerParams(vmem_limit_bytes=8 << 20)
    operands = (cand_grads, val_grads, second_moment)
    odd, rows = projected((3, 5, 7), tables, operands, True, devices)
    odd = back(odd, 1)
    (even,) = projected((2, 4, 6), tables, (rows,), False, devices)
    joined = pl.pallas_call(
        join_kernel,
        out_shape=[jax.ShapeDtypeStruct(even.shape[1:], jnp.float32)] * 3,
        compiler_params=small,
        name="join",
    )(odd, even)
    second = back(joined[1], 2 * apart)
    first = back(joined[0], apart)
    third = back(joined[2], 3 * apart)
    (beside,) = projected((1,), tables, (rows,), False, devices)
    beside = back(beside[0], 1)
    (kept,) = projected((0,), tables, (rows,), False, devices)
    kept = kept[0]

    pairs = groups // 2
    width = first.shape[1]
    cand_part, val_part = pl.pallas_call(
        merge_kernel,
        out_shape=[
            jax.ShapeDtypeStruct((ncand, width), jnp.float32),
            jax.ShapeDtypeStruct((pairs, nval, width), jnp.float32),
        ],
        compiler_params=small,
        name="merge",
    )(beside, kept, first, second, third)
    same_core = [[2 * m + core for m in range(pairs)] for core in range(2)]
    val_own = lax.all_to_all(
        val_part, "cand", 0, 0, tiled=True, axis_index_groups=same_core
    )
    val_other = lax.ppermute(val_own, "cand", [(c, c ^ 1) for c in range(groups)])
    own = groups * nval // devices
    packed = pl.pallas_call(
        dots_kernel,
        out_shape=jax.ShapeDtypeStruct((pairs, 2, own + 8, 128), jnp.float32),
        in_specs=[pl.BlockSpec(memory_space=pltpu.SMEM)] + [pl.BlockSpec()] * 3,
        compiler_params=small,
        name="dots",
    )((lax.axis_index("cand") % 2).reshape(1), cand_part, val_own, val_other)
    packed = packed.reshape(devices, own + 8, 128)
    parts = lax.all_to_all(packed, "feat", 0, 0, tiled=True)
    return pl.pallas_call(
        score_kernel,
        out_shape=jax.ShapeDtypeStruct((own // VPT, ncand), jnp.float32),
        compiler_params=small,
        name="score",
    )(parts).T


def solution(mesh):
    placed = (P("cand", "feat"), P("cand", "feat"), P("feat"), P(), P())
    return jax.shard_map(
        body, mesh=mesh, in_specs=placed, out_specs=P("cand", "feat"), check_vma=False
    )
```

```python
import math

import jax
import jax.numpy as jnp
import numpy as np
from jax import lax
from jax.experimental import pallas as pl
from jax.experimental.pallas import tpu as pltpu
from jax.sharding import PartitionSpec as P


PB = 8192
FB = 64
SLOTS = 8
VPT = 4
GRANT = 32 << 20
SMALL_GRANT = 16 << 20
AHEAD = 2


def wrap32(value):
    value &= 0xFFFFFFFF
    return np.int32(value - (1 << 32) if value >= (1 << 31) else value)


MIX = 73244475
ROW_MUL = wrap32(73856093)
COL_MUL = wrap32(19349663)
MIX_A = wrap32(MIX)
MIX_B = wrap32((MIX << 15) + (1 << 31))


def fold(value):
    return value ^ lax.shift_right_logical(value, jnp.int32(16))


def offset_of(slot, stride):
    return slot * stride if slot % 2 == 0 else (slot - 1) * stride + 1


def project(slots, adam, devices, me_ref, blocks_ref, seeds_ref, *refs):
    if adam:
        cand_hbm, val_hbm, moment_hbm, out_ref, rows_ref, acc_ref, table_ref, cand_ref, moment_ref, sem = refs
    else:
        rows_ref, out_ref, acc_ref, table_ref = refs
    count = len(slots)
    height, length = rows_ref.shape
    blocks = length // PB

    def copies(block):
        at = pl.ds(pl.multiple_of(block * PB, PB), PB)
        ncand = cand_ref.shape[0]
        return (
            pltpu.make_async_copy(moment_hbm.at[:, at], moment_ref.at[:, at], sem.at[0, block]),
            pltpu.make_async_copy(cand_hbm.at[:, at], cand_ref.at[:, at], sem.at[1, block]),
            pltpu.make_async_copy(val_hbm.at[:, at], rows_ref.at[ncand:, at], sem.at[2, block]),
        )

    if adam:
        for block in range(AHEAD):
            for copy in copies(block):
                copy.start()
    me = me_ref[0]
    for n, slot in enumerate(slots):
        owner = lax.rem(me + devices - offset_of(slot, devices // SLOTS), devices)
        for place in range(blocks):
            source = blocks_ref[slot, owner * blocks + place] - me * blocks
            table_ref[0, n, source] = seeds_ref[slot, owner * blocks + place]
            table_ref[1, n, source] = place
    across = fold(lax.broadcasted_iota(jnp.int32, (8, PB), 1) * ROW_MUL)
    column = fold(lax.broadcasted_iota(jnp.int32, (FB, 128), 0) * COL_MUL)
    lane_half = lax.broadcasted_iota(jnp.int32, (height, 2 * FB), 1) // FB

    def one_block(block, carry):
        at = pl.ds(pl.multiple_of(block * PB, PB), PB)
        if adam:

            @pl.when(block + AHEAD < blocks)
            def _():
                for copy in copies(block + AHEAD):
                    copy.start()

            for copy in copies(block):
                copy.wait()
            moment = jnp.broadcast_to(0.999 * moment_ref[:, at], (16, PB))
            for row in range(0, cand_ref.shape[0], 16):
                wide = cand_ref[row : row + 16, at].astype(jnp.float32)
                square = moment + (0.001 * wide) * wide
                den = square * lax.rsqrt(square) + 1e-08
                rows_ref[row : row + 16, at] = (wide * lax.rsqrt(den * den)).astype(jnp.bfloat16)
        mixed = []
        for n in range(count):
            mixed.append(column ^ fold(table_ref[0, n, block]))
        mixed = jnp.concatenate(mixed, axis=0)
        value = jnp.broadcast_to(across[None], (8 * count, 8, PB)).reshape(FB * count, PB)
        value = value ^ jnp.concatenate([mixed] * (PB // 128), axis=1)
        value = fold(value * MIX_A) * MIX_B
        signs = jnp.where(value < 0, jnp.bfloat16(1.0), jnp.bfloat16(-1.0))
        acc = lax.dot_general(
            rows_ref[:, at],
            signs,
            (((1,), (1,)), ((), ())),
            preferred_element_type=jnp.float32,
        )
        if count % 2:
            acc = jnp.concatenate([acc, jnp.zeros((height, FB), jnp.float32)], axis=1)
        for n in range(count):
            place = table_ref[1, n, block]
            half = place % 2
            pair = n // 2 * 2 * FB
            moved = pltpu.roll(acc[:, pair : pair + 2 * FB], (half ^ (n % 2)) * FB, 1)
            acc_ref[n, place // 2] = jnp.where(lane_half == half, moved, acc_ref[n, place // 2])
        return carry

    lax.fori_loop(0, blocks, one_block, 0)
    for n in range(count):
        for pair in range(acc_ref.shape[1]):
            out_ref[n, :, pair * 2 * FB : (pair + 1) * 2 * FB] = acc_ref[n, pair]


def projected(slots, tables, operands, adam, devices):
    count = len(slots)
    smem = pl.BlockSpec(memory_space=pltpu.SMEM)
    vmem = pl.BlockSpec(memory_space=pltpu.VMEM)
    if adam:
        cand, val, moment = operands
        height = cand.shape[0] + val.shape[0]
        length = cand.shape[1]
    else:
        (rows,) = operands
        height, length = rows.shape
    blocks = length // PB
    width = blocks * FB
    out_shape = [jax.ShapeDtypeStruct((count, height, width), jnp.float32)]
    out_specs = [vmem]
    scratch = [
        pltpu.VMEM((count, width // (2 * FB), height, 2 * FB), jnp.float32),
        pltpu.SMEM((2, count, blocks), jnp.int32),
    ]
    if adam:
        out_shape.append(jax.ShapeDtypeStruct((height, length), jnp.bfloat16))
        out_specs.append(vmem)
        scratch += [
            pltpu.VMEM(cand.shape, jnp.bfloat16),
            pltpu.VMEM(moment.shape, jnp.float32),
            pltpu.SemaphoreType.DMA((3, blocks)),
        ]
    return pl.pallas_call(
        lambda *refs: project(slots, adam, devices, *refs),
        out_shape=out_shape,
        in_specs=[smem, smem, smem] + [pl.BlockSpec(memory_space=pltpu.HBM) if adam else vmem] * len(operands),
        out_specs=out_specs,
        scratch_shapes=scratch,
        compiler_params=pltpu.CompilerParams(vmem_limit_bytes=GRANT if adam else SMALL_GRANT),
        cost_estimate=pl.CostEstimate(
            flops=2 * count * width * height * PB * 16,
            bytes_accessed=2 * height * length,
            transcendentals=0,
        ),
        name="project",
    )(*tables, *operands)


def join_kernel(odd_ref, even_ref, *out_refs):
    for n, out_ref in enumerate(out_refs):
        out_ref[...] = odd_ref[n] + even_ref[n]


def merge_kernel(*refs):
    *term_refs, cand_ref, val_ref = refs
    total = term_refs[0][...]
    for term_ref in term_refs[1:]:
        total = total + term_ref[...]
    total = total * (1.0 / math.sqrt(SLOTS * PB))
    ncand = cand_ref.shape[0]
    cand_ref[...] = total[:ncand]
    val_ref[...] = jnp.broadcast_to(total[None, ncand:], val_ref.shape)


def dots_kernel(core_ref, cand_ref, own_ref, other_ref, out_ref):
    cand = cand_ref[...]
    last = (((1,), (1,)), ((), ()))
    ncand = cand.shape[0]
    groups, cores, _, lanes = out_ref.shape
    nval = own_ref.shape[1]
    cand_sq = lax.dot_general(
        jnp.ones((8, cand.shape[1]), jnp.float32),
        cand * cand,
        last,
        precision=lax.Precision.HIGHEST,
        preferred_element_type=jnp.float32,
    )
    squares = jnp.concatenate([cand_sq, jnp.zeros((8, lanes - ncand), jnp.float32)], axis=1)
    val = jnp.concatenate(
        [ref[...].reshape(groups * nval, ref.shape[2]) for ref in (own_ref, other_ref)], axis=0
    )
    dots = lax.dot_general(
        val, cand, last, precision=lax.Precision.HIGHEST, preferred_element_type=jnp.float32
    )
    val_sq = jnp.sum(val * val, axis=1, keepdims=True)
    both = jnp.concatenate([dots, jnp.broadcast_to(val_sq, (val.shape[0], lanes - ncand))], axis=1)
    for swapped in range(cores):
        core = core_ref[0] ^ swapped
        for group in range(groups):
            at = (swapped * groups + group) * nval
            out_ref[group, core, :nval, :] = both[at : at + nval]
            out_ref[group, core, nval:, :] = squares


def score_kernel(parts_ref, out_ref):
    ntask, ncand = out_ref.shape
    own = ntask * VPT
    total = jnp.sum(parts_ref[...], axis=0)
    val_norm = jnp.sqrt(total[:own, ncand : ncand + 1] + 1e-06)
    cand_norm = jnp.sqrt(total[own : own + 1, :ncand] + 1e-06)
    cosine = total[:own, :ncand] / val_norm / cand_norm
    rows = [
        jnp.sum(cosine[task * VPT : (task + 1) * VPT], axis=0, keepdims=True) for task in range(ntask)
    ]
    out_ref[...] = jnp.concatenate(rows, axis=0) / VPT


def body(cand_grads, val_grads, second_moment, slot_blocks, slot_seeds):
    devices = lax.axis_size("feat")
    groups = lax.axis_size("cand")
    ncand = cand_grads.shape[0]
    nval = val_grads.shape[0]

    cand_grads, val_grads, second_moment, slot_blocks, slot_seeds = (
        pltpu.with_memory_space_constraint(x, pltpu.HBM)
        for x in (cand_grads, val_grads, second_moment[None, :], slot_blocks, slot_seeds)
    )
    tables = (lax.axis_index("feat").reshape(1), slot_blocks, slot_seeds)

    def back(part, steps):
        return lax.ppermute(part, "feat", [(j, (j - steps) % devices) for j in range(devices)])

    apart = devices // (SLOTS // 2)
    small = pltpu.CompilerParams(vmem_limit_bytes=8 << 20)
    operands = (cand_grads, val_grads, second_moment)
    odd, rows = projected((3, 5, 7), tables, operands, True, devices)
    odd = back(odd, 1)
    (even,) = projected((2, 4, 6), tables, (rows,), False, devices)
    joined = pl.pallas_call(
        join_kernel,
        out_shape=[jax.ShapeDtypeStruct(even.shape[1:], jnp.float32)] * 3,
        compiler_params=small,
        name="join",
    )(odd, even)
    second = back(joined[1], 2 * apart)
    first = back(joined[0], apart)
    third = back(joined[2], 3 * apart)
    (beside,) = projected((1,), tables, (rows,), False, devices)
    beside = back(beside[0], 1)
    (kept,) = projected((0,), tables, (rows,), False, devices)
    kept = kept[0]

    pairs = groups // 2
    width = first.shape[1]
    cand_part, val_part = pl.pallas_call(
        merge_kernel,
        out_shape=[
            jax.ShapeDtypeStruct((ncand, width), jnp.float32),
            jax.ShapeDtypeStruct((pairs, nval, width), jnp.float32),
        ],
        compiler_params=small,
        name="merge",
    )(beside, kept, first, second, third)
    same_core = [[2 * m + core for m in range(pairs)] for core in range(2)]
    val_own = lax.all_to_all(
        val_part, "cand", 0, 0, tiled=True, axis_index_groups=same_core
    )
    val_other = lax.ppermute(val_own, "cand", [(c, c ^ 1) for c in range(groups)])
    own = groups * nval // devices
    packed = pl.pallas_call(
        dots_kernel,
        out_shape=jax.ShapeDtypeStruct((pairs, 2, own + 8, 128), jnp.float32),
        in_specs=[pl.BlockSpec(memory_space=pltpu.SMEM)] + [pl.BlockSpec()] * 3,
        compiler_params=small,
        name="dots",
    )((lax.axis_index("cand") % 2).reshape(1), cand_part, val_own, val_other)
    packed = packed.reshape(devices, own + 8, 128)
    parts = lax.all_to_all(packed, "feat", 0, 0, tiled=True)
    return pl.pallas_call(
        score_kernel,
        out_shape=jax.ShapeDtypeStruct((own // VPT, ncand), jnp.float32),
        compiler_params=small,
        name="score",
    )(parts).T


def solution(mesh):
    placed = (P("cand", "feat"), P("cand", "feat"), P("feat"), P(), P())
    return jax.shard_map(
        body, mesh=mesh, in_specs=placed, out_specs=P("cand", "feat"), check_vma=False
    )
```
